32 devices in a mesh: groups: 2 (over y), chan: 4 (over z), freq: 2 (over x), win: 2 (over core).
Axes of the slice: x: 2, y: 2, z: 4, core: 2. Of those that a mesh axis runs over, the one named last changes fastest.
Arguments:
- record: bfloat16 [16, 2048, 1000], P(('groups', 'chan', 'win'), 'freq'), parts along dimension 0, may hold values from -50 to 50, as said below
- pair_list: int32 [8192, 2], P(('groups', 'chan')), parts along dimension 0, may hold values from -1 to 2047, as said below
Outputs:
- correlation: float32 [8192, 1000], P(('groups', 'chan', 'freq', 'win')), parts along dimension 0
The draws below stay inside these ranges and needn't reach their ends.
There are 2 independent parts, one for each index of `groups`. The reference program is written for one: setup_inputs(seed, part) draws one part's arguments, and reference() takes and returns one part's arrays. A program takes and returns all parts, laid end to end along the dimension named above; each array names one. Nothing has to cross between parts.
Inputs may be any that keep to these rules, and one draw needn't show every extreme that they name: `record`: channel gains differ strongly from channel to channel. `pair_list`: slot r belongs to block j = r // 1024. A live slot holds a channel of block j (channels j * 512 to (j + 1) * 512 - 1) and a different channel at most 256 positions from it; an empty slot holds -1 twice. Empty slots of a block come after all its live ones; every block has 512 or more live slots and some block has all 1024 live.
All inputs are finite; a program needn't handle non-finite values.
Results may differ from the reference program's by a relative error of at most 0.0052.
Values may be sent and summed in bfloat16 or wider, within the bound.
A program may use at most 64 MiB of HBM per device.

```python
import math
import jax
import jax.numpy as jnp
from jax import lax

SAMPLES = 1000
FFT_LEN = 1024
BINS = 512
LAGS = 1000
SMOOTH = 8
SPAN = 256
CH_BLOCK = 512
PAIR_CAP = 1024
CHANNELS = 2048
WINDOWS = 8


def draw_record(key, part):
    gain_key, noise_key = jax.random.split(key)
    gains = jnp.exp(jax.random.uniform(gain_key, (CHANNELS,), jnp.float32, math.log(0.1), math.log(10.0)))
    noise = jnp.clip(jax.random.normal(noise_key, (WINDOWS, CHANNELS, SAMPLES), jnp.float32), -5.0, 5.0)
    return (noise * gains[None, :, None]).astype(jnp.bfloat16)


def draw_pair_list(key, part):
    keys = jax.random.split(jax.random.fold_in(key, 7), 5)
    blocks = CHANNELS // CH_BLOCK
    first_local = jax.random.randint(keys[0], (blocks, PAIR_CAP), 0, CH_BLOCK)
    first = first_local + jnp.arange(blocks, dtype=jnp.int32)[:, None] * CH_BLOCK
    distance = jax.random.randint(keys[1], (blocks, PAIR_CAP), 1, SPAN + 1)
    sign_bit = jax.random.randint(keys[2], (blocks, PAIR_CAP), 0, 2) * 2 - 1
    offset = distance * sign_bit
    candidate = first + offset
    second = jnp.where((candidate < 0) | (candidate >= CHANNELS), first - offset, candidate)
    live_counts = jax.random.randint(keys[3], (blocks,), PAIR_CAP // 2, PAIR_CAP + 1)
    full_block = jax.random.randint(keys[4], (), 0, blocks)
    live_counts = jnp.where(jnp.arange(blocks) == full_block, PAIR_CAP, live_counts)
    live_slot = jnp.arange(PAIR_CAP)[None, :] < live_counts[:, None]
    first = jnp.where(live_slot, first, -1)
    second = jnp.where(live_slot, second, -1)
    return jnp.stack([first, second], axis=-1).reshape(blocks * PAIR_CAP, 2).astype(jnp.int32)


def setup_inputs(seed: int = 0, part: int = 0) -> dict:
    arg_keys = jax.random.split(jax.random.key(seed), 3)
    part_splits = jax.random.split(jax.random.fold_in(arg_keys[2], part), 3)
    record = draw_record(jax.random.fold_in(jax.random.fold_in(arg_keys[2], part), 71), part)
    pair_list = draw_pair_list(jax.random.fold_in(jax.random.fold_in(arg_keys[2], part), 71), part)
    return dict(record=record, pair_list=pair_list)


floor_level = 0.5

def dft_parts(bin_index):
    samples = jnp.arange(SAMPLES, dtype=jnp.int32)
    angles = jnp.mod(samples[:, None] * bin_index[None, :], FFT_LEN).astype(jnp.float32) * (2.0 * math.pi / FFT_LEN)
    factor = 1.0 / math.sqrt(FFT_LEN)
    return (jnp.cos(angles) * factor, -jnp.sin(angles) * factor)

def lag_columns(bin_index, factor):
    lag_index = jnp.arange(LAGS, dtype=jnp.int32) - LAGS // 2
    angles = jnp.mod(bin_index[:, None] * lag_index[None, :], FFT_LEN).astype(jnp.float32) * (2.0 * math.pi / FFT_LEN)
    return jnp.concatenate([jnp.cos(angles) * factor, -jnp.sin(angles) * factor], axis=0)

def smooth_amplitude(amplitude):
    width = amplitude.shape[-1]
    padded = jnp.pad(amplitude, [(0, 0)] * (amplitude.ndim - 1) + [(SMOOTH, SMOOTH)])
    summed = padded[..., 0:width]
    for step in range(1, 2 * SMOOTH + 1):
        summed = summed + padded[..., step:step + width]
    bins = jnp.arange(1, width + 1, dtype=jnp.int32)
    counts = (jnp.minimum(bins + SMOOTH, width) - jnp.maximum(bins - SMOOTH, 1) + 1).astype(jnp.float32)
    return summed / counts

def whiten(spec_re, spec_im):
    amplitude = jnp.sqrt(spec_re * spec_re + spec_im * spec_im)
    divisor = jnp.maximum(smooth_amplitude(amplitude), floor_level)
    return (spec_re / divisor, spec_im / divisor)

def reference(record, pair_list):
    bin_index = 1 + jnp.arange(BINS, dtype=jnp.int32)
    cos_part, sin_part = dft_parts(bin_index)
    dft_table = jnp.concatenate([cos_part, sin_part], axis=1).astype(jnp.bfloat16)

    def one_window(window):
        spectrum = jnp.dot(window, dft_table, preferred_element_type=jnp.float32)
        white_re, white_im = whiten(spectrum[:, :BINS], spectrum[:, BINS:])
        return jnp.concatenate([white_re, white_im], axis=1).astype(jnp.bfloat16)
    whitened = lax.map(one_window, record)
    live_slot = pair_list[:, 0] >= 0
    left_index = jnp.where(live_slot, pair_list[:, 0], 0).astype(jnp.int32)
    right_index = jnp.where(live_slot, pair_list[:, 1], 0).astype(jnp.int32)
    live_weight = live_slot.astype(jnp.float32)
    slot_total = pair_list.shape[0]
    groups_count = slot_total // PAIR_CAP

    def cross_block(operands):
        left_part, right_part, weight_part = operands
        left_rows = whitened[:, left_part].astype(jnp.float32)
        right_rows = whitened[:, right_part].astype(jnp.float32)
        left_re, left_im = (left_rows[..., :BINS], left_rows[..., BINS:])
        right_re, right_im = (right_rows[..., :BINS], right_rows[..., BINS:])
        cross_re = lax.optimization_barrier(jnp.sum(left_re * right_re + left_im * right_im, axis=0))
        cross_im = lax.optimization_barrier(jnp.sum(left_im * right_re - left_re * right_im, axis=0))
        return jnp.concatenate([cross_re, cross_im], axis=1) * weight_part[:, None]
    cross = lax.map(cross_block, (left_index.reshape(groups_count, PAIR_CAP), right_index.reshape(groups_count, PAIR_CAP), live_weight.reshape(groups_count, PAIR_CAP)))
    cross = cross.reshape(slot_total, 2 * BINS)
    windows = record.shape[0]
    lag_table = lag_columns(bin_index, 1.0 / math.sqrt(windows * BINS))
    return jnp.dot(cross, lag_table, precision=lax.Precision.HIGHEST, preferred_element_type=jnp.float32)
```

```python
import functools
import math

import jax
import jax.numpy as jnp
import numpy as np
from jax import lax
from jax.experimental import pallas as pl
from jax.experimental.pallas import tpu as pltpu
from jax.sharding import PartitionSpec as P

SAMPLES = 1000
FFT_LEN = 1024
BINS = 512
LAGS = 1000
SMOOTH = 8
SPAN = 256
FLOOR = 0.5


def dft_table():
    bins = 1 + np.arange(BINS)
    angles = ((np.arange(SAMPLES)[:, None] * bins[None, :]) % FFT_LEN) * (2.0 * np.pi / FFT_LEN)
    table = np.concatenate([np.cos(angles), -np.sin(angles)], axis=1) / math.sqrt(FFT_LEN)
    return jnp.asarray(table.astype(np.float32)).astype(jnp.bfloat16)


def smoothing():
    bins = np.arange(BINS)
    band = (np.abs(bins[:, None] - bins[None, :]) <= SMOOTH).astype(np.float32)
    return band, (1.0 / band.sum(axis=0, keepdims=True)).astype(np.float32)


def rotation(windows):
    bins = 1 + np.arange(BINS)
    angles = ((bins * (LAGS // 2)) % FFT_LEN) * (2.0 * np.pi / FFT_LEN)
    scale = math.sqrt(FFT_LEN) / math.sqrt(windows * BINS)
    return (np.stack([np.cos(angles), np.sin(angles)]) * scale).astype(np.float32)


def whiten_rows(rows, table, band, inverse):
    spectrum = jnp.dot(rows, table, preferred_element_type=jnp.float32)
    spec_re, spec_im = spectrum[:, :BINS], spectrum[:, BINS:]
    amplitude = jnp.sqrt(spec_re * spec_re + spec_im * spec_im)
    high = amplitude.astype(jnp.bfloat16)
    low = (amplitude - high.astype(jnp.float32)).astype(jnp.bfloat16)
    summed = jnp.dot(high, band, preferred_element_type=jnp.float32) + jnp.dot(
        low, band, preferred_element_type=jnp.float32
    )
    factor = 1.0 / jnp.maximum(summed * inverse, FLOOR)
    return (spec_re * factor).astype(jnp.bfloat16), (spec_im * factor).astype(jnp.bfloat16)


def whiten_kernel(parts, x_ref, table_ref, band_ref, inverse_ref, out_ref):
    count = BINS // parts
    white_re, white_im = whiten_rows(x_ref[...], table_ref[...], band_ref[...], inverse_ref[...])
    for q in range(parts):
        out_ref[q, :, 0:count] = white_re[:, q * count : (q + 1) * count]
        out_ref[q, :, count : 2 * count] = white_im[:, q * count : (q + 1) * count]


def cross_rows(left_index, right_index, block, left_data, right_data, base, rot, wins):
    length = left_data.shape[0]
    reach = right_data.shape[0]
    count = rot.shape[1]
    start = block * length
    own = jnp.logical_and(left_index >= start, left_index < start + length)
    first = jnp.where(own, left_index, right_index) - start
    second = jnp.where(own, right_index, left_index) - base
    sign = jnp.where(own, 1.0, -1.0)
    slots = left_index.shape[0]
    one_left = jnp.where(
        lax.broadcasted_iota(jnp.int32, (slots, length), 1) == first, 1.0, 0.0
    ).astype(jnp.bfloat16)
    one_right = jnp.where(
        lax.broadcasted_iota(jnp.int32, (slots, reach), 1) == second, 1.0, 0.0
    ).astype(jnp.bfloat16)
    left = jnp.dot(one_left, left_data, preferred_element_type=jnp.float32)
    right = jnp.dot(one_right, right_data, preferred_element_type=jnp.float32)
    real = imag = 0.0
    for w in range(wins):
        at = 2 * count * w
        left_re, left_im = left[:, at : at + count], left[:, at + count : at + 2 * count]
        right_re, right_im = right[:, at : at + count], right[:, at + count : at + 2 * count]
        real = real + (left_re * right_re + left_im * right_im)
        imag = imag + (left_im * right_re - left_re * right_im)
    imag = imag * sign
    cosine, sine = rot[0:1], rot[1:2]
    return real * cosine + imag * sine, imag * cosine - real * sine


def cross_kernel(wins, length, reach, tile, pair_ref, data_ref, rot_ref, out_ref):
    block = pl.program_id(0)
    channels = data_ref.shape[0]
    base = pl.multiple_of(
        jnp.clip(block * length - SPAN, 0, channels - reach), math.gcd(SPAN, length)
    )
    start = pl.multiple_of(block * length, length)
    left_data = data_ref[pl.ds(start, length), :]
    right_data = data_ref[pl.ds(base, reach), :]
    count = rot_ref.shape[1]
    for at in range(0, pair_ref.shape[0], tile):
        real, imag = cross_rows(
            pair_ref[at : at + tile, 0:1],
            pair_ref[at : at + tile, 1:2],
            block,
            left_data,
            right_data,
            base,
            rot_ref[...],
            wins,
        )
        out_ref[0, at : at + tile, 0:count] = real.astype(jnp.bfloat16)
        out_ref[0, at : at + tile, count : 2 * count] = imag.astype(jnp.bfloat16)


def exchange(pieces, axes, size):
    me = lax.axis_index(axes)
    out = []
    for step in range(size):
        perm = [(i, i ^ step) for i in range(size)]
        piece = lax.dynamic_index_in_dim(pieces, me ^ step, 0, keepdims=False)
        out.append(piece if step == 0 else lax.ppermute(piece, axes, perm))
    return out


def body(record, pair_list):
    win_local, chan_local, samples = record.shape
    chan_size, freq_size, win_size = (lax.axis_size(a) for a in ("chan", "freq", "win"))
    parts = freq_size * win_size
    axes = ("freq", "win")
    count = BINS // parts
    windows = win_local * chan_size * win_size
    channels = chan_local * freq_size
    length = channels // chan_size
    reach = length + 2 * SPAN
    slots = pair_list.shape[0]
    me = lax.axis_index(axes)
    table = dft_table()
    band, inverse = smoothing()
    tile = 256
    whitened = pl.pallas_call(
        functools.partial(whiten_kernel, parts),
        grid=(chan_local // tile,),
        in_specs=[
            pl.BlockSpec((tile, samples), lambda i: (i, 0)),
            pl.BlockSpec((samples, 2 * BINS), lambda i: (0, 0)),
            pl.BlockSpec((BINS, BINS), lambda i: (0, 0)),
            pl.BlockSpec((1, BINS), lambda i: (0, 0)),
        ],
        out_specs=pl.BlockSpec((parts, tile, 2 * count), lambda i: (0, i, 0)),
        out_shape=jax.ShapeDtypeStruct((parts, chan_local, 2 * count), jnp.bfloat16),
    )(record.reshape(chan_local, samples), table, jnp.asarray(band, jnp.bfloat16), inverse)
    pairs = lax.all_gather(pair_list, "chan", axis=0, tiled=True)
    if parts & (parts - 1) == 0:
        got = exchange(whitened, axes, parts)
    stacked = jnp.stack(got)
    order = jnp.arange(parts) ^ me
    data = jnp.take(stacked, order, axis=0)
    data = data.reshape(freq_size, win_size, chan_local, 2 * count)
    data = data.transpose(0, 2, 1, 3).reshape(channels, win_size * 2 * count)
    rot = jnp.asarray(rotation(windows)).reshape(2, parts, count)
    rot = lax.dynamic_index_in_dim(rot, me, 1, keepdims=False)
    cross = pl.pallas_call(
        functools.partial(cross_kernel, win_size, length, reach, tile),
        grid=(chan_size,),
        in_specs=[
            pl.BlockSpec((slots, 2), lambda i: (i, 0)),
            pl.BlockSpec((channels, win_size * 2 * count), lambda i: (0, 0)),
            pl.BlockSpec((2, count), lambda i: (0, 0)),
        ],
        out_specs=pl.BlockSpec((1, slots, 2 * count), lambda i: (i, 0, 0)),
        out_shape=jax.ShapeDtypeStruct((chan_size, slots, 2 * count), jnp.bfloat16),
    )(pairs, data, rot)
    c = lax.axis_index("chan")

    def block_of(d):
        return lax.dynamic_index_in_dim(cross, jnp.clip(d, 0, chan_size - 1), 0, keepdims=False)

    right = left = None
    for t in range(1, chan_size):
        send_right = block_of(chan_size - t + c)
        send_left = block_of(t - chan_size + c)
        if right is not None:
            send_right = (send_right.astype(jnp.float32) + right.astype(jnp.float32)).astype(
                jnp.bfloat16
            )
            send_left = (send_left.astype(jnp.float32) + left.astype(jnp.float32)).astype(
                jnp.bfloat16
            )
        right = lax.ppermute(send_right, "chan", [(i, i + 1) for i in range(t)])
        left = lax.ppermute(
            send_left, "chan", [(i, i - 1) for i in range(chan_size - 1, chan_size - 1 - t, -1)]
        )
    total = block_of(c).astype(jnp.float32)
    total = (total + right.astype(jnp.float32) + left.astype(jnp.float32)).astype(jnp.bfloat16)
    final = exchange(total.reshape(parts, slots // parts, 2 * count), axes, parts)
    final = jnp.take(jnp.stack(final), order, axis=0)
    final = final.reshape(parts, slots // parts, 2, count).transpose(1, 2, 0, 3)
    final = final.reshape(slots // parts, 2 * BINS)
    return lax.dot_general(
        final, table, (((1,), (1,)), ((), ())), preferred_element_type=jnp.float32
    )


def solution(mesh):
    in_specs = (P(("groups", "chan", "win"), "freq", None), P(("groups", "chan"), None))
    out_specs = P(("groups", "chan", "freq", "win"), None)
    return jax.shard_map(body, mesh=mesh, in_specs=in_specs, out_specs=out_specs, check_vma=False)
```

```python
import functools
import math

import jax
import jax.numpy as jnp
import numpy as np
from jax import lax
from jax.experimental import pallas as pl
from jax.experimental.pallas import tpu as pltpu
from jax.sharding import PartitionSpec as P

SAMPLES = 1000
FFT_LEN = 1024
BINS = 512
LAGS = 1000
SMOOTH = 8
SPAN = 256
FLOOR = 0.5


def dft_table():
    bins = 1 + np.arange(BINS)
    angles = ((np.arange(SAMPLES)[:, None] * bins[None, :]) % FFT_LEN) * (2.0 * np.pi / FFT_LEN)
    table = np.concatenate([np.cos(angles), -np.sin(angles)], axis=1) / math.sqrt(FFT_LEN)
    return jnp.asarray(table.astype(np.float32)).astype(jnp.bfloat16)


def smoothing():
    bins = np.arange(BINS)
    band = (np.abs(bins[:, None] - bins[None, :]) <= SMOOTH).astype(np.float32)
    return band, (1.0 / band.sum(axis=0, keepdims=True)).astype(np.float32)


def rotation(windows):
    bins = 1 + np.arange(BINS)
    angles = ((bins * (LAGS // 2)) % FFT_LEN) * (2.0 * np.pi / FFT_LEN)
    scale = math.sqrt(FFT_LEN) / math.sqrt(windows * BINS)
    return (np.stack([np.cos(angles), np.sin(angles)]) * scale).astype(np.float32)


def whiten_rows(rows, table, band, inverse):
    spectrum = jnp.dot(rows, table, preferred_element_type=jnp.float32)
    spec_re, spec_im = spectrum[:, :BINS], spectrum[:, BINS:]
    amplitude = jnp.sqrt(spec_re * spec_re + spec_im * spec_im)
    high = amplitude.astype(jnp.bfloat16)
    low = (amplitude - high.astype(jnp.float32)).astype(jnp.bfloat16)
    summed = jnp.dot(high, band, preferred_element_type=jnp.float32) + jnp.dot(
        low, band, preferred_element_type=jnp.float32
    )
    factor = 1.0 / jnp.maximum(summed * inverse, FLOOR)
    return (spec_re * factor).astype(jnp.bfloat16), (spec_im * factor).astype(jnp.bfloat16)


def cross_rows(left_index, right_index, start, base, left_data, right_data, rot):
    length = left_data[0].shape[0]
    reach = right_data[0].shape[0]
    count = rot.shape[1]
    own = jnp.logical_and(left_index >= start, left_index < start + length)
    first = jnp.where(own, left_index, right_index) - start
    second = jnp.where(own, right_index, left_index) - base
    sign = jnp.where(own, 1.0, -1.0)
    slots = left_index.shape[0]
    one_left = jnp.where(
        lax.broadcasted_iota(jnp.int32, (slots, length), 1) == first, 1.0, 0.0
    ).astype(jnp.bfloat16)
    one_right = jnp.where(
        lax.broadcasted_iota(jnp.int32, (slots, reach), 1) == second, 1.0, 0.0
    ).astype(jnp.bfloat16)
    real = imag = 0.0
    for left_window, right_window in zip(left_data, right_data):
        left = jnp.dot(one_left, left_window, preferred_element_type=jnp.float32)
        right = jnp.dot(one_right, right_window, preferred_element_type=jnp.float32)
        left_re, left_im = left[:, :count], left[:, count:]
        right_re, right_im = right[:, :count], right[:, count:]
        real = real + (left_re * right_re + left_im * right_im)
        imag = imag + (left_im * right_re - left_re * right_im)
    imag = imag * sign
    cosine, sine = rot[0:1], rot[1:2]
    return real * cosine + imag * sine, imag * cosine - real * sine


def fused_kernel(
    chunk,
    tiles,
    x_ref,
    pair_ref,
    table_ref,
    band_ref,
    inverse_ref,
    rot_ref,
    out_ref,
    white,
    data,
    pairs,
    cross,
    from_left,
    from_right,
    final,
    total,
    pair_send,
    pair_recv,
    white_send,
    white_recv,
    right_send,
    right_recv,
    left_send,
    left_recv,
    final_send,
    final_recv,
):
    chans, freqs, wins = (lax.axis_size(a) for a in ("chan", "freq", "win"))
    parts = freqs * wins
    count = BINS // parts
    c, f, w = (lax.axis_index(a) for a in ("chan", "freq", "win"))
    me = f * wins + w
    rows = x_ref.shape[1]
    channels = rows * freqs
    length = channels // chans
    reach = length + 2 * SPAN
    slots = pair_ref.shape[1]
    tile = slots // tiles
    piece = slots // parts
    per_tile = parts // tiles
    mesh_id = pl.DeviceIdType.MESH

    def part_id(q):
        return {"freq": q // wins, "win": q % wins}

    def ahead(step):
        return lax.rem(me + step, parts)

    barrier = pltpu.get_barrier_semaphore()
    for step in range(1, parts):
        pl.semaphore_signal(barrier, 1, device_id=part_id(ahead(step)), device_id_type=mesh_id)
    for step in range(1, chans):
        pl.semaphore_signal(
            barrier, 1, device_id={"chan": lax.rem(c + step, chans)}, device_id_type=mesh_id
        )
    pl.semaphore_wait(barrier, parts - 1 + chans - 1)

    def pair_copy(step):
        return pltpu.make_async_remote_copy(
            src_ref=pair_ref,
            dst_ref=pairs.at[c],
            send_sem=pair_send.at[step],
            recv_sem=pair_recv.at[step],
            device_id={"chan": lax.rem(c + step, chans)},
            device_id_type=mesh_id,
        )

    for step in range(1, chans):
        pair_copy(step).start()
    pairs[c] = pair_ref[...]

    def white_copy(at, step):
        row = pl.multiple_of(at * chunk, chunk)
        place = pl.multiple_of(f * rows + at * chunk, chunk)
        return pltpu.make_async_remote_copy(
            src_ref=white.at[ahead(step), pl.ds(row, chunk)],
            dst_ref=data.at[w, pl.ds(place, chunk)],
            send_sem=white_send.at[at, step],
            recv_sem=white_recv.at[at, step],
            device_id=part_id(ahead(step)),
            device_id_type=mesh_id,
        )

    @pl.loop(0, rows // chunk)
    def _(at):
        row = pl.multiple_of(at * chunk, chunk)
        place = pl.multiple_of(f * rows + at * chunk, chunk)
        white_re, white_im = whiten_rows(
            x_ref[0, pl.ds(row, chunk), :], table_ref[...], band_ref[...], inverse_ref[...]
        )
        for q in range(parts):
            white[q, pl.ds(row, chunk), 0:count] = white_re[:, q * count : (q + 1) * count]
            white[q, pl.ds(row, chunk), count : 2 * count] = white_im[
                :, q * count : (q + 1) * count
            ]
        for step in range(1, parts):
            white_copy(at, step).start()
        data[w, pl.ds(place, chunk), :] = white[me, pl.ds(row, chunk), :]

    for step in range(1, chans):
        pair_copy(step).wait()

    @pl.loop(0, rows // chunk)
    def _(at):
        for step in range(1, parts):
            white_copy(at, step).wait()

    def own_tile(block, k):
        at = pl.multiple_of(k * tile, tile)
        index = jnp.transpose(pairs[block, :, pl.ds(at, tile)])
        base = pl.multiple_of(
            jnp.clip(block * length - SPAN, 0, channels - reach), math.gcd(SPAN, length)
        )
        start = pl.multiple_of(block * length, length)
        return cross_rows(
            index[:, 0:1],
            index[:, 1:2],
            start,
            base,
            [data[v, pl.ds(start, length), :] for v in range(wins)],
            [data[v, pl.ds(base, reach), :] for v in range(wins)],
            rot_ref[...],
        )

    def line_copy(t, k, block, buffer, send, recv, target):
        at = pl.multiple_of(k * tile, tile)
        return pltpu.make_async_remote_copy(
            src_ref=cross.at[block, pl.ds(at, tile)],
            dst_ref=buffer.at[t - 1, pl.ds(at, tile)],
            send_sem=send.at[t - 1, k],
            recv_sem=recv.at[t - 1, k],
            device_id={"chan": target},
            device_id_type=mesh_id,
        )

    def right_copy(t, k):
        block = jnp.clip(chans - t + c, 0, chans - 1)
        return line_copy(
            t, k, block, from_left, right_send, right_recv, lax.rem(c + 1, chans)
        )

    def left_copy(t, k):
        block = jnp.clip(t - chans + c, 0, chans - 1)
        return line_copy(
            t, k, block, from_right, left_send, left_recv, lax.rem(c + chans - 1, chans)
        )

    mirror = chans - 1 - c

    def one_way(t, k, place, block, copy, buffer):
        @pl.when(place < t)
        def _():
            at = pl.multiple_of(k * tile, tile)
            real, imag = own_tile(block, k)
            partial = jnp.concatenate([real, imag], axis=1)

            @pl.when(place == 0)
            def _():
                cross[block, pl.ds(at, tile), :] = partial.astype(jnp.bfloat16)

            @pl.when(place > 0)
            def _():
                copy(t - 1, k).wait_recv()
                arrived = buffer[t - 2, pl.ds(at, tile), :].astype(jnp.float32)
                cross[block, pl.ds(at, tile), :] = (partial + arrived).astype(jnp.bfloat16)

            copy(t, k).start()

    @pl.loop(1, chans)
    def _(t):
        @pl.loop(0, tiles)
        def _(k):
            right_block = jnp.clip(chans - t + c, 0, chans - 1)
            left_block = jnp.clip(t - chans + c, 0, chans - 1)
            one_way(t, k, c, right_block, right_copy, from_left)
            one_way(t, k, mirror, left_block, left_copy, from_right)

    def final_copy(q):
        step = lax.rem(q - me + parts, parts)
        return pltpu.make_async_remote_copy(
            src_ref=total.at[pl.ds(pl.multiple_of(q * piece, piece), piece)],
            dst_ref=final.at[me],
            send_sem=final_send.at[step],
            recv_sem=final_recv.at[step],
            device_id=part_id(q),
            device_id_type=mesh_id,
        )

    @pl.loop(0, tiles)
    def _(k):
        at = pl.multiple_of(k * tile, tile)
        real, imag = own_tile(c, k)
        cross[c, pl.ds(at, tile), 0:count] = real.astype(jnp.bfloat16)
        cross[c, pl.ds(at, tile), count : 2 * count] = imag.astype(jnp.bfloat16)

    @pl.loop(0, tiles)
    def _(k):
        at = pl.multiple_of(k * tile, tile)

        total[pl.ds(at, tile), :] = cross[c, pl.ds(at, tile), :]
        for place, copy, buffer in ((c, right_copy, from_left), (mirror, left_copy, from_right)):

            @pl.when(place > 0)
            def _():
                copy(chans - 1, k).wait_recv()
                total[pl.ds(at, tile), :] = (
                    total[pl.ds(at, tile), :].astype(jnp.float32)
                    + buffer[chans - 2, pl.ds(at, tile), :].astype(jnp.float32)
                ).astype(jnp.bfloat16)

        for extra in range(per_tile):
            q = k * per_tile + extra

            @pl.when(q != me)
            def _():
                final_copy(q).start()

            @pl.when(q == me)
            def _():
                final[me] = total[pl.ds(pl.multiple_of(q * piece, piece), piece), :]

    @pl.loop(1, chans)
    def _(t):
        @pl.loop(0, tiles)
        def _(k):
            @pl.when(c < t)
            def _():
                right_copy(t, k).wait_send()

            @pl.when(mirror < t)
            def _():
                left_copy(t, k).wait_send()

    for step in range(1, parts):
        final_copy(ahead(step)).wait()
    for q in range(parts):
        out_ref[:, q * count : (q + 1) * count] = final[q, :, 0:count]
        out_ref[:, BINS + q * count : BINS + (q + 1) * count] = final[q, :, count : 2 * count]


def body(record, pair_list):
    win_local, rows, samples = record.shape
    chans, freqs, wins = (lax.axis_size(a) for a in ("chan", "freq", "win"))
    parts = freqs * wins
    count = BINS // parts
    channels = rows * freqs
    slots = pair_list.shape[0]
    me = lax.axis_index(("freq", "win"))
    table = dft_table()
    band, inverse = smoothing()
    rot = jnp.asarray(rotation(win_local * chans * wins)).reshape(2, parts, count)
    rot = lax.dynamic_index_in_dim(rot, me, 1, keepdims=False)
    listed = jnp.pad(pair_list.T, ((0, 6), (0, 0)))
    tiles = min(4, parts)
    chunk = 256
    chunks = rows // chunk
    vmem = pl.BlockSpec(memory_space=pltpu.VMEM)
    dma = pltpu.SemaphoreType.DMA
    half = jnp.bfloat16
    final = pl.pallas_call(
        functools.partial(fused_kernel, chunk, tiles),
        in_specs=[vmem] * 6,
        out_specs=vmem,
        out_shape=jax.ShapeDtypeStruct((slots // parts, 2 * BINS), half),
        scratch_shapes=[
            pltpu.VMEM((parts, rows, 2 * count), half),
            pltpu.VMEM((wins, channels, 2 * count), half),
            pltpu.VMEM((chans, 8, slots), jnp.int32),
            pltpu.VMEM((chans, slots, 2 * count), half),
            pltpu.VMEM((chans - 1, slots, 2 * count), half),
            pltpu.VMEM((chans - 1, slots, 2 * count), half),
            pltpu.VMEM((parts, slots // parts, 2 * count), half),
            pltpu.VMEM((slots, 2 * count), half),
            dma((chans,)),
            dma((chans,)),
            dma((chunks, parts)),
            dma((chunks, parts)),
            dma((chans - 1, tiles)),
            dma((chans - 1, tiles)),
            dma((chans - 1, tiles)),
            dma((chans - 1, tiles)),
            dma((parts,)),
            dma((parts,)),
        ],
        compiler_params=pltpu.CompilerParams(
            collective_id=0, has_side_effects=True, vmem_limit_bytes=60000 * 1024
        ),
    )(record, listed, table, jnp.asarray(band, half), jnp.asarray(inverse), rot)
    return lax.dot_general(
        final, table, (((1,), (1,)), ((), ())), preferred_element_type=jnp.float32
    )


def solution(mesh):
    in_specs = (P(("groups", "chan", "win"), "freq", None), P(("groups", "chan"), None))
    out_specs = P(("groups", "chan", "freq", "win"), None)
    return jax.shard_map(body, mesh=mesh, in_specs=in_specs, out_specs=out_specs, check_vma=False)
```

```python
import functools
import math

import jax
import jax.numpy as jnp
import numpy as np
from jax import lax
from jax.experimental import pallas as pl
from jax.experimental.pallas import tpu as pltpu
from jax.sharding import PartitionSpec as P

SAMPLES = 1000
FFT_LEN = 1024
BINS = 512
LAGS = 1000
SMOOTH = 8
SPAN = 256
FLOOR = 0.5


def dft_table():
    bins = 1 + np.arange(BINS)
    angles = ((bins[:, None] * np.arange(SAMPLES)[None, :]) % FFT_LEN) * (2.0 * np.pi / FFT_LEN)
    table = np.concatenate([np.cos(angles), -np.sin(angles)], axis=0) / math.sqrt(FFT_LEN)
    return jnp.asarray(table.astype(np.float32)).astype(jnp.bfloat16)


def per_bin(windows):
    bins = np.arange(BINS)
    band = (np.abs(bins[:, None] - bins[None, :]) <= SMOOTH).astype(np.float32)
    angles = (((1 + bins) * (LAGS // 2)) % FFT_LEN) * (2.0 * np.pi / FFT_LEN)
    scale = math.sqrt(FFT_LEN) / math.sqrt(windows * BINS)
    columns = np.zeros((BINS, 128), np.float32)
    columns[:, 0] = np.cos(angles) * scale
    columns[:, 1] = np.sin(angles) * scale
    columns[:, 2] = 1.0 / band.sum(axis=1)
    return jnp.asarray(band).astype(jnp.bfloat16), jnp.asarray(columns)


def whiten_columns(samples, table, band, inverse):
    spectrum = jnp.dot(table, samples, preferred_element_type=jnp.float32)
    spec_re, spec_im = spectrum[:BINS], spectrum[BINS:]
    amplitude = jnp.sqrt(spec_re * spec_re + spec_im * spec_im)
    high = amplitude.astype(jnp.bfloat16)
    low = (amplitude - high.astype(jnp.float32)).astype(jnp.bfloat16)
    summed = jnp.dot(band, high, preferred_element_type=jnp.float32) + jnp.dot(
        band, low, preferred_element_type=jnp.float32
    )
    factor = 1.0 / jnp.maximum(summed * inverse, FLOOR)
    return (spec_re * factor).astype(jnp.bfloat16), (spec_im * factor).astype(jnp.bfloat16)


def cross_columns(left_index, right_index, start, base, left_data, right_data, cosine, sine):
    length = left_data[0].shape[1]
    reach = right_data[0].shape[1]
    count = cosine.shape[0]
    own = jnp.logical_and(left_index >= start, left_index < start + length)
    first = jnp.where(own, left_index, right_index) - start
    second = jnp.where(own, right_index, left_index) - base
    sign = jnp.where(own, 1.0, -1.0)
    slots = left_index.shape[1]
    one_left = jnp.where(
        lax.broadcasted_iota(jnp.int32, (length, slots), 0) == first, 1.0, 0.0
    ).astype(jnp.bfloat16)
    one_right = jnp.where(
        lax.broadcasted_iota(jnp.int32, (reach, slots), 0) == second, 1.0, 0.0
    ).astype(jnp.bfloat16)
    real = imag = 0.0
    for left_window, right_window in zip(left_data, right_data):
        left = jnp.dot(left_window, one_left, preferred_element_type=jnp.float32)
        right = jnp.dot(right_window, one_right, preferred_element_type=jnp.float32)
        left_re, left_im = left[:count], left[count:]
        right_re, right_im = right[:count], right[count:]
        real = real + (left_re * right_re + left_im * right_im)
        imag = imag + (left_im * right_re - left_re * right_im)
    imag = imag * sign
    return jnp.concatenate(
        [real * cosine + imag * sine, imag * cosine - real * sine], axis=0
    )


def fused_kernel(
    chunk,
    tiles,
    x_ref,
    pair_ref,
    table_ref,
    band_ref,
    bin_ref,
    out_ref,
    white,
    data,
    pairs,
    cross,
    from_left,
    from_right,
    final,
    total,
    pair_send,
    pair_recv,
    white_send,
    white_recv,
    right_send,
    right_recv,
    left_send,
    left_recv,
    final_send,
    final_recv,
):
    chans, freqs, wins = (lax.axis_size(a) for a in ("chan", "freq", "win"))
    parts = freqs * wins
    count = BINS // parts
    c, f, w = (lax.axis_index(a) for a in ("chan", "freq", "win"))
    me = f * wins + w
    rows = x_ref.shape[2]
    chunks = rows // chunk
    channels = rows * freqs
    length = channels // chans
    reach = length + 2 * SPAN
    slots = pair_ref.shape[1]
    tile = slots // tiles
    piece = slots // parts
    per_tile = parts // tiles
    mesh_id = pl.DeviceIdType.MESH
    last = chans - 1
    mirror = last - c

    def part_id(q):
        return {"freq": q // wins, "win": q % wins}

    def partner(step):
        far, near = step // wins, step % wins
        return lax.rem(f + far, freqs) * wins + lax.rem(w + near, wins)

    barrier = pltpu.get_barrier_semaphore()
    for step in range(1, parts):
        pl.semaphore_signal(barrier, 1, device_id=part_id(partner(step)), device_id_type=mesh_id)
    for step in range(1, chans):
        pl.semaphore_signal(
            barrier, 1, device_id={"chan": lax.rem(c + step, chans)}, device_id_type=mesh_id
        )
    pl.semaphore_wait(barrier, parts - 1 + chans - 1)

    def pair_copy(step):
        return pltpu.make_async_remote_copy(
            src_ref=pair_ref,
            dst_ref=pairs.at[c],
            send_sem=pair_send.at[step],
            recv_sem=pair_recv.at[step],
            device_id={"chan": lax.rem(c + step, chans)},
            device_id_type=mesh_id,
        )

    for step in range(1, chans):
        pair_copy(step).start()
    pairs[c] = pair_ref[...]

    def chunk_at(i):
        return (1 - f) * (chunks - 1 - i) + f * i if freqs == 2 else i

    def white_copy(i, step):
        return pltpu.make_async_remote_copy(
            src_ref=white.at[i, partner(step)],
            dst_ref=data.at[w, f * chunks + chunk_at(i)],
            send_sem=white_send.at[i, step],
            recv_sem=white_recv.at[i, step],
            device_id=part_id(partner(step)),
            device_id_type=mesh_id,
        )

    @pl.loop(0, chunks)
    def _(i):
        column = pl.multiple_of(chunk_at(i) * chunk, chunk)
        white_re, white_im = whiten_columns(
            x_ref[0, :, pl.ds(column, chunk)], table_ref[...], band_ref[...], bin_ref[:, 2:3]
        )
        for q in range(parts):
            white[i, q, 0:count, :] = white_re[q * count : (q + 1) * count]
            white[i, q, count : 2 * count, :] = white_im[q * count : (q + 1) * count]
        for step in reversed(range(1, parts)):
            white_copy(i, step).start()
        data[w, f * chunks + chunk_at(i)] = white[i, me]

    for step in range(1, chans):
        pair_copy(step).wait()
    near_steps = [s for s in range(1, parts) if s < wins]
    far_steps = [s for s in range(1, parts) if s >= wins]

    @pl.loop(0, chunks)
    def _(i):
        for step in near_steps:
            white_copy(i, step).wait()

    def needed(block):
        if freqs != 2:
            return chunks
        top = min(max(block * length - SPAN, 0), channels - reach) + reach
        return min(max(-(-(top - rows) // chunk), 0), chunks)

    own_bins = pl.ds(pl.multiple_of(me * count, count), count)

    def own_tile(block, k):
        at = pl.multiple_of(k * tile, tile)
        base = jnp.clip(block * length - SPAN, 0, channels - reach)
        start = block * length
        low, high = start // chunk, base // chunk
        return cross_columns(
            pairs[block, 0:1, pl.ds(at, tile)],
            pairs[block, 1:2, pl.ds(at, tile)],
            start,
            base,
            [
                jnp.concatenate([data[v, low + i] for i in range(length // chunk)], axis=1)
                for v in range(wins)
            ],
            [
                jnp.concatenate([data[v, high + i] for i in range(reach // chunk)], axis=1)
                for v in range(wins)
            ],
            bin_ref[own_bins, 0:1],
            bin_ref[own_bins, 1:2],
        )

    def right_copy(block, k):
        return pltpu.make_async_remote_copy(
            src_ref=cross.at[block, k],
            dst_ref=from_left.at[block, k],
            send_sem=right_send.at[block, k],
            recv_sem=right_recv.at[block, k],
            device_id={"chan": lax.rem(c + 1, chans)},
            device_id_type=mesh_id,
        )

    def left_copy(block, k):
        return pltpu.make_async_remote_copy(
            src_ref=cross.at[block, k],
            dst_ref=from_right.at[block, k],
            send_sem=left_send.at[block, k],
            recv_sem=left_recv.at[block, k],
            device_id={"chan": lax.rem(c + last, chans)},
            device_id_type=mesh_id,
        )

    def one_way(active, place, block, k, copy, buffer):
        @pl.when(active)
        def _():
            partial = own_tile(block, k)

            @pl.when(place == 0)
            def _():
                cross[block, k] = partial.astype(jnp.bfloat16)

            @pl.when(place > 0)
            def _():
                copy(block, k).wait_recv()
                arrived = buffer[block, k].astype(jnp.float32)
                cross[block, k] = (partial + arrived).astype(jnp.bfloat16)

            copy(block, k).start()

    upper = jnp.where(f > 0, 1, 0) if freqs == 2 else 1

    def line_step(t):
        right_block = (1 - upper) * (t - c) + upper * (chans - t + c)
        left_turned = upper * (t - mirror) + (1 - upper) * (chans - t + mirror)
        if freqs != 2:
            left_turned = chans - t + mirror
        right_on = jnp.logical_and(right_block > c, right_block < chans)
        left_on = jnp.logical_and(left_turned > mirror, left_turned < chans)
        right_block = jnp.clip(right_block, 0, last)
        left_block = jnp.clip(last - left_turned, 0, last)

        @pl.loop(0, tiles)
        def _(k):
            one_way(right_on, c, right_block, k, right_copy, from_left)
            one_way(left_on, mirror, left_block, k, left_copy, from_right)

    waited = 0
    if freqs == 2:
        steps = 2 * chans - 3
        for t in range(1, steps + 1):
            more = chunks if t >= last else needed(t)
            for i in range(waited, more):
                for step in far_steps:
                    white_copy(i, step).wait()
            waited = max(waited, more)
            line_step(t)
    else:

        @pl.loop(0, chunks)
        def _(i):
            for step in far_steps:
                white_copy(i, step).wait()

        pl.loop(1, chans)(line_step)

    def final_copy(q):
        turn = lax.rem(q // wins - f + freqs, freqs) * wins + lax.rem(q % wins - w + wins, wins)
        return pltpu.make_async_remote_copy(
            src_ref=total.at[q],
            dst_ref=final.at[me],
            send_sem=final_send.at[turn],
            recv_sem=final_recv.at[turn],
            device_id=part_id(q),
            device_id_type=mesh_id,
        )

    @pl.loop(0, tiles)
    def _(k):
        cross[c, k] = own_tile(c, k).astype(jnp.bfloat16)

    @pl.loop(0, tiles)
    def _(k):
        for place, copy, buffer in ((c, right_copy, from_left), (mirror, left_copy, from_right)):

            @pl.when(place > 0)
            def _():
                copy(c, k).wait_recv()
                cross[c, k] = (
                    cross[c, k].astype(jnp.float32) + buffer[c, k].astype(jnp.float32)
                ).astype(jnp.bfloat16)

        summed = cross[c, k]
        for extra in range(per_tile):
            q = k * per_tile + extra
            total[q] = summed[:, extra * piece : (extra + 1) * piece]

            @pl.when(q != me)
            def _():
                final_copy(q).start()

            @pl.when(q == me)
            def _():
                final[me] = total[q]

    @pl.loop(0, chans)
    def _(block):
        @pl.loop(0, tiles)
        def _(k):
            @pl.when(block > c)
            def _():
                right_copy(block, k).wait_send()

            @pl.when(block < c)
            def _():
                left_copy(block, k).wait_send()

    for step in range(1, parts):
        final_copy(partner(step)).wait()
    for q in range(parts):
        out_ref[q * count : (q + 1) * count, :] = final[q, 0:count, :]
        out_ref[BINS + q * count : BINS + (q + 1) * count, :] = final[q, count : 2 * count, :]


def body(record, pair_list):
    win_local, rows, samples = record.shape
    chans, freqs, wins = (lax.axis_size(a) for a in ("chan", "freq", "win"))
    parts = freqs * wins
    count = BINS // parts
    slots = pair_list.shape[0]
    table = dft_table()
    band, columns = per_bin(win_local * chans * wins)
    tiles = min(4, parts)
    chunk = 256
    chunks = rows // chunk
    piece = slots // parts
    vmem = pl.BlockSpec(memory_space=pltpu.VMEM)
    dma = pltpu.SemaphoreType.DMA
    half = jnp.bfloat16
    line = pltpu.VMEM((chans, tiles, 2 * count, slots // tiles), half)
    final = pl.pallas_call(
        functools.partial(fused_kernel, chunk, tiles),
        in_specs=[vmem] * 5,
        out_specs=vmem,
        out_shape=jax.ShapeDtypeStruct((2 * BINS, piece), half),
        scratch_shapes=[
            pltpu.VMEM((chunks, parts, 2 * count, chunk), half),
            pltpu.VMEM((wins, freqs * chunks, 2 * count, chunk), half),
            pltpu.VMEM((chans, 2, slots), jnp.int32),
            line,
            line,
            line,
            pltpu.VMEM((parts, 2 * count, piece), half),
            pltpu.VMEM((parts, 2 * count, piece), half),
            dma((chans,)),
            dma((chans,)),
            dma((chunks, parts)),
            dma((chunks, parts)),
            dma((chans, tiles)),
            dma((chans, tiles)),
            dma((chans, tiles)),
            dma((chans, tiles)),
            dma((parts,)),
            dma((parts,)),
        ],
        compiler_params=pltpu.CompilerParams(
            collective_id=0, has_side_effects=True, vmem_limit_bytes=60000 * 1024
        ),
    )(jnp.swapaxes(record, 1, 2), pair_list.T, table, band, columns)
    lags = lax.dot_general(
        table, final, (((0,), (0,)), ((), ())), preferred_element_type=jnp.float32
    )
    return lags.T


def solution(mesh):
    in_specs = (P(("groups", "chan", "win"), "freq", None), P(("groups", "chan"), None))
    out_specs = P(("groups", "chan", "freq", "win"), None)
    return jax.shard_map(body, mesh=mesh, in_specs=in_specs, out_specs=out_specs, check_vma=False)
```

```python
import functools
import math

import jax
import jax.numpy as jnp
import numpy as np
from jax import lax
from jax.experimental import pallas as pl
from jax.experimental.pallas import tpu as pltpu
from jax.sharding import PartitionSpec as P

SAMPLES = 1000
FFT_LEN = 1024
BINS = 512
LAGS = 1000
SMOOTH = 8
SPAN = 256
FLOOR = 0.5


def dft_table():
    bins = 1 + np.arange(BINS)
    angles = ((bins[:, None] * np.arange(SAMPLES)[None, :]) % FFT_LEN) * (2.0 * np.pi / FFT_LEN)
    table = np.concatenate([np.cos(angles), -np.sin(angles)], axis=0) / math.sqrt(FFT_LEN)
    return jnp.asarray(table.astype(np.float32)).astype(jnp.bfloat16)


def per_bin(windows):
    bins = np.arange(BINS)
    band = (np.abs(bins[:, None] - bins[None, :]) <= SMOOTH).astype(np.float32)
    angles = (((1 + bins) * (LAGS // 2)) % FFT_LEN) * (2.0 * np.pi / FFT_LEN)
    scale = math.sqrt(FFT_LEN) / math.sqrt(windows * BINS)
    columns = np.zeros((BINS, 128), np.float32)
    columns[:, 0] = np.cos(angles) * scale
    columns[:, 1] = np.sin(angles) * scale
    columns[:, 2] = 1.0 / band.sum(axis=1)
    return jnp.asarray(band).astype(jnp.bfloat16), jnp.asarray(columns)


def whiten_columns(samples, table, band, inverse):
    spectrum = jnp.dot(table, samples, preferred_element_type=jnp.float32)
    spec_re, spec_im = spectrum[:BINS], spectrum[BINS:]
    amplitude = jnp.sqrt(spec_re * spec_re + spec_im * spec_im)
    high = amplitude.astype(jnp.bfloat16)
    low = (amplitude - high.astype(jnp.float32)).astype(jnp.bfloat16)
    summed = jnp.dot(band, high, preferred_element_type=jnp.float32) + jnp.dot(
        band, low, preferred_element_type=jnp.float32
    )
    factor = 1.0 / jnp.maximum(summed * inverse, FLOOR)
    return (spec_re * factor).astype(jnp.bfloat16), (spec_im * factor).astype(jnp.bfloat16)


def cross_columns(left_index, right_index, start, base, left_data, right_data, cosine, sine):
    length = left_data[0].shape[1]
    reach = right_data[0].shape[1]
    count = cosine.shape[0]
    own = jnp.logical_and(left_index >= start, left_index < start + length)
    first = jnp.where(own, left_index, right_index) - start
    second = jnp.where(own, right_index, left_index) - base
    sign = jnp.where(own, 1.0, -1.0)
    slots = left_index.shape[1]
    one_left = jnp.where(
        lax.broadcasted_iota(jnp.int32, (length, slots), 0) == first, 1.0, 0.0
    ).astype(jnp.bfloat16)
    one_right = jnp.where(
        lax.broadcasted_iota(jnp.int32, (reach, slots), 0) == second, 1.0, 0.0
    ).astype(jnp.bfloat16)
    real = imag = 0.0
    for left_window, right_window in zip(left_data, right_data):
        left = jnp.dot(left_window, one_left, preferred_element_type=jnp.float32)
        right = jnp.dot(right_window, one_right, preferred_element_type=jnp.float32)
        left_re, left_im = left[:count], left[count:]
        right_re, right_im = right[:count], right[count:]
        real = real + (left_re * right_re + left_im * right_im)
        imag = imag + (left_im * right_re - left_re * right_im)
    imag = imag * sign
    return jnp.concatenate(
        [real * cosine + imag * sine, imag * cosine - real * sine], axis=0
    )


def fused_kernel(
    chunk,
    tiles,
    split,
    x_ref,
    pair_ref,
    table_ref,
    band_ref,
    bin_ref,
    out_ref,
    white,
    data,
    pairs,
    cross,
    from_left,
    from_right,
    final,
    total,
    pair_send,
    pair_recv,
    white_send,
    white_recv,
    right_send,
    right_recv,
    left_send,
    left_recv,
    final_send,
    final_recv,
):
    chans, freqs, wins = (lax.axis_size(a) for a in ("chan", "freq", "win"))
    parts = freqs * wins
    count = BINS // parts
    c, f, w = (lax.axis_index(a) for a in ("chan", "freq", "win"))
    me = f * wins + w
    rows = x_ref.shape[2]
    chunks = rows // chunk
    channels = rows * freqs
    length = channels // chans
    reach = length + 2 * SPAN
    slots = pair_ref.shape[1]
    tile = slots // tiles
    piece = slots // parts
    per_tile = parts // tiles
    mesh_id = pl.DeviceIdType.MESH
    last = chans - 1
    slice_rows = 2 * count // split
    mirror = last - c

    def part_id(q):
        return {"freq": q // wins, "win": q % wins}

    def partner(step):
        far, near = step // wins, step % wins
        return lax.rem(f + far, freqs) * wins + lax.rem(w + near, wins)

    barrier = pltpu.get_barrier_semaphore()
    for step in range(1, parts):
        pl.semaphore_signal(barrier, 1, device_id=part_id(partner(step)), device_id_type=mesh_id)
    for step in range(1, chans):
        pl.semaphore_signal(
            barrier, 1, device_id={"chan": lax.rem(c + step, chans)}, device_id_type=mesh_id
        )
    pl.semaphore_wait(barrier, parts - 1 + chans - 1)

    def pair_copy(step):
        return pltpu.make_async_remote_copy(
            src_ref=pair_ref,
            dst_ref=pairs.at[c],
            send_sem=pair_send.at[step],
            recv_sem=pair_recv.at[step],
            device_id={"chan": lax.rem(c + step, chans)},
            device_id_type=mesh_id,
        )

    for step in range(1, chans):
        pair_copy(step).start()
    pairs[c] = pair_ref[...]

    def chunk_at(i):
        return (1 - f) * (chunks - 1 - i) + f * i if freqs == 2 else i

    def white_copy(i, step):
        return pltpu.make_async_remote_copy(
            src_ref=white.at[i, partner(step)],
            dst_ref=data.at[w, f * chunks + chunk_at(i)],
            send_sem=white_send.at[i, step],
            recv_sem=white_recv.at[i, step],
            device_id=part_id(partner(step)),
            device_id_type=mesh_id,
        )

    @pl.loop(0, chunks)
    def _(i):
        column = pl.multiple_of(chunk_at(i) * chunk, chunk)
        white_re, white_im = whiten_columns(
            x_ref[0, :, pl.ds(column, chunk)], table_ref[...], band_ref[...], bin_ref[:, 2:3]
        )
        for q in range(parts):
            white[i, q, 0:count, :] = white_re[q * count : (q + 1) * count]
            white[i, q, count : 2 * count, :] = white_im[q * count : (q + 1) * count]
        for step in reversed(range(1, parts)):
            white_copy(i, step).start()
        data[w, f * chunks + chunk_at(i)] = white[i, me]

    for step in range(1, chans):
        pair_copy(step).wait()
    near_steps = [s for s in range(1, parts) if s < wins]
    far_steps = [s for s in range(1, parts) if s >= wins]

    @pl.loop(0, chunks)
    def _(i):
        for step in near_steps:
            white_copy(i, step).wait()

    def needed(block):
        if freqs != 2:
            return chunks
        top = min(max(block * length - SPAN, 0), channels - reach) + reach
        return min(max(-(-(top - rows) // chunk), 0), chunks)

    own_bins = pl.ds(pl.multiple_of(me * count, count), count)

    def own_tile(block, k):
        at = pl.multiple_of(k * tile, tile)
        base = jnp.clip(block * length - SPAN, 0, channels - reach)
        start = block * length
        low, high = start // chunk, base // chunk
        return cross_columns(
            pairs[block, 0:1, pl.ds(at, tile)],
            pairs[block, 1:2, pl.ds(at, tile)],
            start,
            base,
            [
                jnp.concatenate([data[v, low + i] for i in range(length // chunk)], axis=1)
                for v in range(wins)
            ],
            [
                jnp.concatenate([data[v, high + i] for i in range(reach // chunk)], axis=1)
                for v in range(wins)
            ],
            bin_ref[own_bins, 0:1],
            bin_ref[own_bins, 1:2],
        )

    def right_copy(block, k, h):
        return pltpu.make_async_remote_copy(
            src_ref=cross.at[block, k, pl.ds(h * slice_rows, slice_rows)],
            dst_ref=from_left.at[block, k, pl.ds(h * slice_rows, slice_rows)],
            send_sem=right_send.at[block, k * split + h],
            recv_sem=right_recv.at[block, k * split + h],
            device_id={"chan": lax.rem(c + 1, chans)},
            device_id_type=mesh_id,
        )

    def left_copy(block, k, h):
        return pltpu.make_async_remote_copy(
            src_ref=cross.at[block, k, pl.ds(h * slice_rows, slice_rows)],
            dst_ref=from_right.at[block, k, pl.ds(h * slice_rows, slice_rows)],
            send_sem=left_send.at[block, k * split + h],
            recv_sem=left_recv.at[block, k * split + h],
            device_id={"chan": lax.rem(c + last, chans)},
            device_id_type=mesh_id,
        )

    def one_way(active, place, block, k, copy, buffer):
        @pl.when(active)
        def _():
            partial = own_tile(block, k)
            for h in range(split):
                lines = slice(h * slice_rows, (h + 1) * slice_rows)
                mine = partial[lines]

                @pl.when(place == 0)
                def _():
                    cross[block, k, lines, :] = mine.astype(jnp.bfloat16)

                @pl.when(place > 0)
                def _():
                    copy(block, k, h).wait_recv()
                    arrived = buffer[block, k, lines, :].astype(jnp.float32)
                    cross[block, k, lines, :] = (mine + arrived).astype(jnp.bfloat16)

                copy(block, k, h).start()

    upper = jnp.where(f > 0, 1, 0) if freqs == 2 else 1

    def line_step(t):
        right_block = (1 - upper) * (t - c) + upper * (chans - t + c)
        left_turned = upper * (t - mirror) + (1 - upper) * (chans - t + mirror)
        if freqs != 2:
            left_turned = chans - t + mirror
        right_on = jnp.logical_and(right_block > c, right_block < chans)
        left_on = jnp.logical_and(left_turned > mirror, left_turned < chans)
        right_block = jnp.clip(right_block, 0, last)
        left_block = jnp.clip(last - left_turned, 0, last)

        @pl.loop(0, tiles)
        def _(k):
            one_way(right_on, c, right_block, k, right_copy, from_left)
            one_way(left_on, mirror, left_block, k, left_copy, from_right)

    waited = 0
    if freqs == 2:
        steps = 2 * chans - 3
        for t in range(1, steps + 1):
            more = chunks if t >= last else needed(t)
            for i in range(waited, more):
                for step in far_steps:
                    white_copy(i, step).wait()
            waited = max(waited, more)
            line_step(t)
    else:

        @pl.loop(0, chunks)
        def _(i):
            for step in far_steps:
                white_copy(i, step).wait()

        pl.loop(1, chans)(line_step)

    def final_copy(q):
        turn = lax.rem(q // wins - f + freqs, freqs) * wins + lax.rem(q % wins - w + wins, wins)
        return pltpu.make_async_remote_copy(
            src_ref=total.at[q],
            dst_ref=final.at[me],
            send_sem=final_send.at[turn],
            recv_sem=final_recv.at[turn],
            device_id=part_id(q),
            device_id_type=mesh_id,
        )

    @pl.loop(0, tiles)
    def _(k):
        cross[c, k] = own_tile(c, k).astype(jnp.bfloat16)

    @pl.loop(0, tiles)
    def _(k):
        for place, copy, buffer in ((c, right_copy, from_left), (mirror, left_copy, from_right)):

            @pl.when(place > 0)
            def _():
                for h in range(split):
                    copy(c, k, h).wait_recv()
                cross[c, k] = (
                    cross[c, k].astype(jnp.float32) + buffer[c, k].astype(jnp.float32)
                ).astype(jnp.bfloat16)

        summed = cross[c, k]
        for extra in range(per_tile):
            q = k * per_tile + extra
            total[q] = summed[:, extra * piece : (extra + 1) * piece]

            @pl.when(q != me)
            def _():
                final_copy(q).start()

            @pl.when(q == me)
            def _():
                final[me] = total[q]

    @pl.loop(0, chans)
    def _(block):
        @pl.loop(0, tiles)
        def _(k):
            @pl.when(block > c)
            def _():
                for h in range(split):
                    right_copy(block, k, h).wait_send()

            @pl.when(block < c)
            def _():
                for h in range(split):
                    left_copy(block, k, h).wait_send()

    for step in range(1, parts):
        final_copy(partner(step)).wait()
    for q in range(parts):
        out_ref[q * count : (q + 1) * count, :] = final[q, 0:count, :]
        out_ref[BINS + q * count : BINS + (q + 1) * count, :] = final[q, count : 2 * count, :]


def body(record, pair_list):
    win_local, rows, samples = record.shape
    chans, freqs, wins = (lax.axis_size(a) for a in ("chan", "freq", "win"))
    parts = freqs * wins
    count = BINS // parts
    slots = pair_list.shape[0]
    table = dft_table()
    band, columns = per_bin(win_local * chans * wins)
    tiles = min(4, parts)
    split = max(1, 16 // chans)
    chunk = 256
    chunks = rows // chunk
    piece = slots // parts
    vmem = pl.BlockSpec(memory_space=pltpu.VMEM)
    dma = pltpu.SemaphoreType.DMA
    half = jnp.bfloat16
    line = pltpu.VMEM((chans, tiles, 2 * count, slots // tiles), half)
    final = pl.pallas_call(
        functools.partial(fused_kernel, chunk, tiles, split),
        in_specs=[vmem] * 5,
        out_specs=vmem,
        out_shape=jax.ShapeDtypeStruct((2 * BINS, piece), half),
        scratch_shapes=[
            pltpu.VMEM((chunks, parts, 2 * count, chunk), half),
            pltpu.VMEM((wins, freqs * chunks, 2 * count, chunk), half),
            pltpu.VMEM((chans, 2, slots), jnp.int32),
            line,
            line,
            line,
            pltpu.VMEM((parts, 2 * count, piece), half),
            pltpu.VMEM((parts, 2 * count, piece), half),
            dma((chans,)),
            dma((chans,)),
            dma((chunks, parts)),
            dma((chunks, parts)),
            dma((chans, tiles * split)),
            dma((chans, tiles * split)),
            dma((chans, tiles * split)),
            dma((chans, tiles * split)),
            dma((parts,)),
            dma((parts,)),
        ],
        compiler_params=pltpu.CompilerParams(
            collective_id=0, has_side_effects=True, vmem_limit_bytes=60000 * 1024
        ),
    )(jnp.swapaxes(record, 1, 2), pair_list.T, table, band, columns)
    lags = lax.dot_general(
        table, final, (((0,), (0,)), ((), ())), preferred_element_type=jnp.float32
    )
    return lags.T


def solution(mesh):
    in_specs = (P(("groups", "chan", "win"), "freq", None), P(("groups", "chan"), None))
    out_specs = P(("groups", "chan", "freq", "win"), None)
    return jax.shard_map(body, mesh=mesh, in_specs=in_specs, out_specs=out_specs, check_vma=False)
```
